32 devices in a mesh: tgt: 16 (over z, y, x), src: 2 (over core).
Axes of the slice: x: 2, y: 2, z: 4, core: 2. Of those that a mesh axis runs over, the one named last changes fastest.
Arguments:
- node_feats: bfloat16 [4096, 128], P(('tgt', 'src')), may hold values from -6 to 6
- tile_index: int32 [16, 2, 8], P('tgt', 'src'), may hold values from 0 to 31, as said below
- tile_count: int32 [16, 2], P('tgt', 'src'), may hold values from 1 to 8
- tile_vals: float32 [16, 2, 8, 128, 128], P('tgt', 'src'), may hold values from -0.375 to 0.375
- w_in: bfloat16 [128, 512], replicated, may hold values from -0.5 to 0.5
- w_out: bfloat16 [512, 172], replicated, may hold values from -0.25 to 0.25
Outputs:
- logits: float32 [4096, 172], P(('tgt', 'src'))
The draws below stay inside these ranges and needn't reach their ends.
Inputs may be any that keep to these rules, and one draw needn't show every extreme that they name: `tile_index`: within one block pair the slots' entries are distinct.
All inputs are finite; a program needn't handle non-finite values.
Results may differ from the reference program's by a relative error of at most 0.005.
Values may be sent and summed in bfloat16 or wider, within the bound.
No kernel may reach another device: no remote copies, remote signals or barrier semaphores. Data moves between devices by JAX's collectives and lax.ppermute only.
A program may use at most 64 MiB of HBM per device.

```python
import jax
import jax.numpy as jnp
from jax import lax

FEAT_IN = 128
HIDDEN_SIZE = 512
CLASSES = 172
TILE = 128
NODE_DEV = 128
NODES = 4096
ROW_TILES = 2
COL_TILES = 16
SLOTS = 8
N_TGT = 16
N_SRC = 2


def draw_tile_index(key, part):
    total = N_TGT * N_SRC
    keys = jax.random.split(jax.random.fold_in(key, 7), total)
    picks = jax.vmap(lambda one_key: jax.random.permutation(one_key, ROW_TILES * COL_TILES)[:SLOTS])(keys)
    return picks.reshape(N_TGT, N_SRC, SLOTS).astype(jnp.int32)


def draw_tile_count(key, part):
    total = N_TGT * N_SRC
    first_key, second_key = jax.random.split(jax.random.fold_in(key, 11))
    full_slots = jax.random.randint(first_key, (total,), 0, 4) == 0
    partial_slots = jax.random.randint(second_key, (total,), SLOTS // 4, SLOTS // 2 + 1)
    counts = jnp.where(full_slots, SLOTS, jnp.clip(partial_slots, 1, SLOTS))
    counts = counts.at[0].set(SLOTS)
    return counts.reshape(N_TGT, N_SRC).astype(jnp.int32)


def shard_levels(rng, extent, cuts, low, top_value):
    def one(dim, shards_of):
        heights = jax.random.uniform(jax.random.fold_in(jax.random.fold_in(rng, 6), dim), (shards_of,), jnp.float32, low / len(cuts), top_value / len(cuts))
        return jnp.repeat(jnp.exp(heights), extent[dim] // shards_of).reshape((-1,) + (1,) * (len(extent) - dim - 1))

    factor_of = one(*cuts[0])
    for cut in cuts[1:]:
        factor_of = factor_of * one(*cut)
    return factor_of


def scatter_about(stream_key, extent, spread, most, cuts=(), kind=jnp.bfloat16):
    level = shard_levels(stream_key, extent, cuts, -0.22, 0.18) if cuts else 1.0
    values = jax.random.normal(stream_key, extent, jnp.float32) * spread * level
    return jnp.minimum(jnp.maximum(values, -most), most).astype(kind)


def setup_inputs(seed: int = 0) -> dict:
    streams_of = jax.random.split(jax.random.key(seed), 7)
    node_feats = scatter_about(streams_of[0], (NODES, FEAT_IN), 1.0, 6.0, ((0, 32),))
    tile_index = draw_tile_index(jax.random.fold_in(streams_of[6], 71), 0)
    tile_count = draw_tile_count(jax.random.fold_in(streams_of[6], 71), 0)
    tile_vals = scatter_about(streams_of[3], (N_TGT, N_SRC, SLOTS, TILE, TILE), (max(TILE * SLOTS // (2 * ROW_TILES), TILE // 2)) ** -0.5, 0.375, ((0, 16), (1, 2)), jnp.float32)
    w_in = scatter_about(streams_of[4], (FEAT_IN, HIDDEN_SIZE), FEAT_IN ** -0.5, 0.5)
    w_out = scatter_about(streams_of[5], (HIDDEN_SIZE, CLASSES), HIDDEN_SIZE ** -0.5, 0.25)
    return dict(node_feats=node_feats, tile_index=tile_index, tile_count=tile_count, tile_vals=tile_vals, w_in=w_in, w_out=w_out)


def aggregate(tile_block, slot_index, slot_count, source, row_tiles, col_tiles):
    tile_size = tile_block.shape[-1]
    features = source.reshape(col_tiles, tile_size, -1).astype(jnp.float32)
    tile_rows = slot_index // col_tiles
    tile_cols = slot_index % col_tiles
    picked = features[tile_cols]
    live_mask = (jnp.arange(tile_block.shape[0]) < slot_count).astype(jnp.float32)
    products = jnp.einsum("kij,kjf->kif", tile_block, picked, precision=lax.Precision.HIGHEST)
    placing = (tile_rows[:, None] == jnp.arange(row_tiles)[None, :]).astype(jnp.float32) * live_mask[:, None]
    summed = jnp.einsum("kr,kif->rif", placing, products, precision=lax.Precision.HIGHEST)
    return summed.reshape(row_tiles * tile_size, -1)


def propagate(features, tile_index, tile_count, tile_vals):
    width = features.shape[1]
    blocks = features.reshape(N_TGT, N_SRC, NODE_DEV, width).transpose(1, 0, 2, 3)
    blocks = blocks.reshape(N_SRC, N_TGT * NODE_DEV, width)

    def one_target(target):
        totals = jnp.zeros((ROW_TILES * TILE, width), jnp.float32)
        for source_id in range(N_SRC):
            totals = totals + aggregate(tile_vals[target, source_id], tile_index[target, source_id], tile_count[target, source_id], blocks[source_id], ROW_TILES, COL_TILES)
        return totals

    result = lax.map(one_target, jnp.arange(N_TGT))
    return result.reshape(N_TGT * ROW_TILES * TILE, width)


def reference(node_feats, tile_index, tile_count, tile_vals, w_in, w_out):
    agg = propagate(node_feats, tile_index, tile_count, tile_vals).astype(jnp.bfloat16)
    hidden = jax.nn.relu(jnp.dot(agg, w_in, preferred_element_type=jnp.float32)).astype(jnp.bfloat16)
    message = jnp.dot(hidden, w_out, preferred_element_type=jnp.float32).astype(jnp.bfloat16)
    return propagate(message, tile_index, tile_count, tile_vals)
```

```python
import functools

import jax
import jax.numpy as jnp
from jax import lax
from jax.experimental import pallas as pl
from jax.experimental.pallas import tpu as pltpu
from jax.sharding import PartitionSpec as P


VMEM = pl.BlockSpec(memory_space=pltpu.VMEM)
SMEM = pl.BlockSpec(memory_space=pltpu.SMEM)
DIRECT = 4


def place_kernel(row_tiles, code_ref, tiles_ref, w_in_ref, high_ref, low_ref, w_in_t_ref):
    slots, tile, _ = tiles_ref.shape
    for slot in range(slots):
        values = tiles_ref[slot]
        high = values.astype(jnp.bfloat16)
        low = (values - high.astype(jnp.float32)).astype(jnp.bfloat16)
        code = jnp.full((tile, tile), code_ref[slot], jnp.int32)
        columns = slice(slot * tile, (slot + 1) * tile)
        for row in range(row_tiles):
            rows = slice(row * tile, (row + 1) * tile)
            here = code == row
            high_ref[rows, columns] = jnp.where(here, high.astype(jnp.float32), 0.0).astype(jnp.bfloat16)
            low_ref[rows, columns] = jnp.where(here, low.astype(jnp.float32), 0.0).astype(jnp.bfloat16)
    w_in_t_ref[...] = w_in_ref[...].T


def pick(spot_ref, pieces, joined_ref, picked_ref, tile):
    base = 0
    for piece in pieces:
        joined_ref[base : base + piece.shape[0], :] = piece[...]
        base += piece.shape[0]
    for slot in range(picked_ref.shape[0] // tile):
        start = pl.multiple_of(spot_ref[slot] * tile, tile)
        picked_ref[slot * tile : (slot + 1) * tile, :] = joined_ref[pl.ds(start, tile), :]


def first_kernel(count, tile, spot_ref, high_ref, low_ref, *refs):
    pieces, outs = refs[:count], refs[count:-2]
    joined_ref, picked_ref = refs[-2:]
    pick(spot_ref, pieces, joined_ref, picked_ref, tile)
    picked = picked_ref[...]
    own = outs[0].shape[0]
    for d, out in enumerate(outs):
        rows = slice(d * own, (d + 1) * own)
        out[...] = jnp.dot(high_ref[rows, :], picked, preferred_element_type=jnp.float32) + jnp.dot(
            low_ref[rows, :], picked, preferred_element_type=jnp.float32
        )


def times_transposed(left, right):
    return lax.dot_general(left, right, (((1,), (1,)), ((), ())), preferred_element_type=jnp.float32)


def second_kernel(count, tile, spot_ref, high_ref, low_ref, w_in_t_ref, w_out_t_ref, *refs):
    pieces, outs = refs[:count], refs[count:-2]
    joined_ref, picked_ref = refs[-2:]
    pick(spot_ref, pieces, joined_ref, picked_ref, tile)
    hidden = jnp.maximum(times_transposed(w_in_t_ref[...], picked_ref[...]), 0.0).astype(jnp.bfloat16)
    message = jnp.dot(w_out_t_ref[...], hidden, preferred_element_type=jnp.float32).astype(jnp.bfloat16)
    own = outs[0].shape[1]
    for d, out in enumerate(outs):
        rows = slice(d * own, (d + 1) * own)
        out[...] = times_transposed(message, high_ref[rows, :]) + times_transposed(message, low_ref[rows, :])


def exchange(value, groups):
    size = len(groups[0])
    if size > DIRECT or size & (size - 1):
        whole = lax.all_gather(value, "tgt", axis=0, axis_index_groups=groups)
        return [whole[i] for i in range(size)]
    moved = [value]
    for bit in range(1, size):
        pairs = [(group[i], group[i ^ bit]) for group in groups for i in range(size)]
        moved.append(lax.ppermute(value, "tgt", pairs))
    return moved


def spread(value, inner, outer):
    across = [[o * inner + i for o in range(outer)] for i in range(inner)]
    within = [[o * inner + i for i in range(inner)] for o in range(outer)]
    column = jnp.concatenate(exchange(value, across), 0)
    return exchange(column, within)


def place_of(size, mine, wanted):
    if size > DIRECT or size & (size - 1):
        return wanted
    return wanted ^ mine


def to_owner(parts, n_src):
    total = parts[0]
    for d in range(1, n_src):
        pairs = [(i, (i + d) % n_src) for i in range(n_src)]
        total = total + lax.ppermute(parts[d], "src", pairs)
    return total


def shards(node_feats, tile_index, tile_count, tile_vals, w_in, w_out):
    tiles = tile_vals[0, 0]
    slots, tile, _ = tiles.shape
    own, width = node_feats.shape
    classes = w_out.shape[1]
    n_src, n_tgt = lax.axis_size("src"), lax.axis_size("tgt")
    row_tiles, col_tiles = own * n_src // tile, own * n_tgt // tile
    per_own = own // tile
    inner = 1 << ((n_tgt.bit_length() - 1) // 2)
    outer = n_tgt // inner

    index, count = tile_index[0, 0], tile_count[0, 0]
    mine_t, mine_s = lax.axis_index("tgt"), lax.axis_index("src")
    turned = (index // col_tiles + row_tiles - mine_s * per_own) % row_tiles
    code = jnp.where(jnp.arange(slots) < count, turned, -1).astype(jnp.int32)
    column = index % col_tiles
    node, part = column // per_own, column % per_own
    in_spot = place_of(inner, mine_t % inner, node % inner)
    out_spot = place_of(outer, mine_t // inner, node // inner)
    spot = ((in_spot * outer + out_spot) * per_own + part).astype(jnp.int32)

    pieces = spread(node_feats, inner, outer)
    placed = jax.ShapeDtypeStruct((row_tiles * tile, slots * tile), jnp.bfloat16)
    high, low, w_in_t = pl.pallas_call(
        functools.partial(place_kernel, row_tiles),
        out_shape=[placed, placed, jax.ShapeDtypeStruct(w_in.shape[::-1], w_in.dtype)],
        in_specs=[SMEM, VMEM, VMEM],
        out_specs=[VMEM] * 3,
    )(code, tiles, w_in)
    scratch = [
        pltpu.VMEM((own * n_tgt, width), jnp.bfloat16),
        pltpu.VMEM((slots * tile, width), jnp.bfloat16),
    ]
    parts = pl.pallas_call(
        functools.partial(first_kernel, len(pieces), tile),
        out_shape=[jax.ShapeDtypeStruct((own, width), jnp.float32)] * n_src,
        in_specs=[SMEM] + [VMEM] * (2 + len(pieces)),
        out_specs=[VMEM] * n_src,
        scratch_shapes=scratch,
    )(spot, high, low, *pieces)
    agg = to_owner(parts, n_src).astype(jnp.bfloat16)
    pieces = spread(agg, inner, outer)
    parts = pl.pallas_call(
        functools.partial(second_kernel, len(pieces), tile),
        out_shape=[jax.ShapeDtypeStruct((classes, own), jnp.float32)] * n_src,
        in_specs=[SMEM] + [VMEM] * (4 + len(pieces)),
        out_specs=[VMEM] * n_src,
        scratch_shapes=scratch,
    )(spot, high, low, w_in_t, w_out.T, *pieces)
    return to_owner(parts, n_src).T


def solution(mesh):
    in_specs = (
        P(("tgt", "src"), None),
        P("tgt", "src", None),
        P("tgt", "src"),
        P("tgt", "src", None, None, None),
        P(),
        P(),
    )
    out_specs = P(("tgt", "src"), None)
    return jax.shard_map(shards, mesh=mesh, in_specs=in_specs, out_specs=out_specs, check_vma=False)
```

```python
import functools

import jax
import jax.numpy as jnp
from jax import lax
from jax.experimental import pallas as pl
from jax.experimental.pallas import tpu as pltpu
from jax.sharding import PartitionSpec as P


VMEM = pl.BlockSpec(memory_space=pltpu.VMEM)
SMEM = pl.BlockSpec(memory_space=pltpu.SMEM)
DIRECT = 4
GRANT = pltpu.CompilerParams(vmem_limit_bytes=24 << 20)


def inside(*arrays):
    return [pltpu.with_memory_space_constraint(array, pltpu.VMEM) for array in arrays]


def place_kernel(row_tiles, code_ref, tiles_ref, w_in_ref, high_ref, low_ref, w_in_t_ref):
    slots, tile, _ = tiles_ref.shape
    for slot in range(slots):
        values = tiles_ref[slot]
        high = values.astype(jnp.bfloat16)
        low = (values - high.astype(jnp.float32)).astype(jnp.bfloat16)
        code = jnp.full((tile, tile), code_ref[slot], jnp.int32)
        columns = slice(slot * tile, (slot + 1) * tile)
        for row in range(row_tiles):
            rows = slice(row * tile, (row + 1) * tile)
            here = code == row
            high_ref[rows, columns] = jnp.where(here, high.astype(jnp.float32), 0.0).astype(jnp.bfloat16)
            low_ref[rows, columns] = jnp.where(here, low.astype(jnp.float32), 0.0).astype(jnp.bfloat16)
    w_in_t_ref[...] = w_in_ref[...].T


def pick(spot_ref, pieces, joined_ref, picked_ref, tile):
    base = 0
    for piece in pieces:
        joined_ref[base : base + piece.shape[0], :] = piece[...]
        base += piece.shape[0]
    for slot in range(picked_ref.shape[0] // tile):
        start = pl.multiple_of(spot_ref[slot] * tile, tile)
        picked_ref[slot * tile : (slot + 1) * tile, :] = joined_ref[pl.ds(start, tile), :]


def first_kernel(count, tile, spot_ref, high_ref, low_ref, *refs):
    pieces, outs = refs[:count], refs[count:-2]
    joined_ref, picked_ref = refs[-2:]
    pick(spot_ref, pieces, joined_ref, picked_ref, tile)
    picked = picked_ref[...]
    own = outs[0].shape[0]
    for d, out in enumerate(outs):
        rows = slice(d * own, (d + 1) * own)
        out[...] = jnp.dot(high_ref[rows, :], picked, preferred_element_type=jnp.float32) + jnp.dot(
            low_ref[rows, :], picked, preferred_element_type=jnp.float32
        )


def times_transposed(left, right):
    return lax.dot_general(left, right, (((1,), (1,)), ((), ())), preferred_element_type=jnp.float32)


def second_kernel(count, tile, spot_ref, high_ref, low_ref, w_in_t_ref, w_out_t_ref, *refs):
    pieces, outs = refs[:count], refs[count:-2]
    joined_ref, picked_ref = refs[-2:]
    pick(spot_ref, pieces, joined_ref, picked_ref, tile)
    hidden = jnp.maximum(times_transposed(w_in_t_ref[...], picked_ref[...]), 0.0).astype(jnp.bfloat16)
    message = jnp.dot(w_out_t_ref[...], hidden, preferred_element_type=jnp.float32).astype(jnp.bfloat16)
    own = outs[0].shape[1]
    for d, out in enumerate(outs):
        rows = slice(d * own, (d + 1) * own)
        out[...] = times_transposed(message, high_ref[rows, :]) + times_transposed(message, low_ref[rows, :])


def exchange(value, groups):
    size = len(groups[0])
    if size > DIRECT or size & (size - 1):
        whole = lax.all_gather(value, "tgt", axis=0, axis_index_groups=groups)
        return [whole[i] for i in range(size)]
    moved = [value]
    for bit in range(1, size):
        pairs = [(group[i], group[i ^ bit]) for group in groups for i in range(size)]
        moved.append(lax.ppermute(value, "tgt", pairs))
    return moved


def spread(value, inner, outer):
    across = [[o * inner + i for o in range(outer)] for i in range(inner)]
    within = [[o * inner + i for i in range(inner)] for o in range(outer)]
    column = jnp.concatenate(exchange(value, across), 0)
    return exchange(column, within)


def place_of(size, mine, wanted):
    if size > DIRECT or size & (size - 1):
        return wanted
    return wanted ^ mine


def to_owner(parts, n_src):
    total = parts[0]
    for d in range(1, n_src):
        pairs = [(i, (i + d) % n_src) for i in range(n_src)]
        total = total + lax.ppermute(parts[d], "src", pairs)
    return total


def shards(node_feats, tile_index, tile_count, tile_vals, w_in, w_out):
    tiles = tile_vals[0, 0]
    slots, tile, _ = tiles.shape
    own, width = node_feats.shape
    classes = w_out.shape[1]
    n_src, n_tgt = lax.axis_size("src"), lax.axis_size("tgt")
    row_tiles, col_tiles = own * n_src // tile, own * n_tgt // tile
    per_own = own // tile
    inner = 1 << ((n_tgt.bit_length() - 1) // 2)
    outer = n_tgt // inner

    index, count = tile_index[0, 0], tile_count[0, 0]
    mine_t, mine_s = lax.axis_index("tgt"), lax.axis_index("src")
    turned = (index // col_tiles + row_tiles - mine_s * per_own) % row_tiles
    code = jnp.where(jnp.arange(slots) < count, turned, -1).astype(jnp.int32)
    column = index % col_tiles
    node, part = column // per_own, column % per_own
    in_spot = place_of(inner, mine_t % inner, node % inner)
    out_spot = place_of(outer, mine_t // inner, node // inner)
    spot = ((in_spot * outer + out_spot) * per_own + part).astype(jnp.int32)

    pieces = spread(node_feats, inner, outer)
    placed = pltpu.VMEM((row_tiles * tile, slots * tile), jnp.bfloat16)
    high, low, w_in_t = pl.pallas_call(
        functools.partial(place_kernel, row_tiles),
        out_shape=[placed, placed, pltpu.VMEM(w_in.shape[::-1], w_in.dtype)],
        in_specs=[SMEM, VMEM, VMEM],
        out_specs=[VMEM] * 3,
        compiler_params=GRANT,
    )(code, *inside(tiles, w_in))
    scratch = [
        pltpu.VMEM((own * n_tgt, width), jnp.bfloat16),
        pltpu.VMEM((slots * tile, width), jnp.bfloat16),
    ]
    parts = pl.pallas_call(
        functools.partial(first_kernel, len(pieces), tile),
        out_shape=[pltpu.VMEM((own, width), jnp.float32)] * n_src,
        in_specs=[SMEM] + [VMEM] * (2 + len(pieces)),
        out_specs=[VMEM] * n_src,
        scratch_shapes=scratch,
        compiler_params=GRANT,
    )(spot, *inside(high, low, *pieces))
    agg = to_owner(parts, n_src).astype(jnp.bfloat16)
    pieces = spread(agg, inner, outer)
    parts = pl.pallas_call(
        functools.partial(second_kernel, len(pieces), tile),
        out_shape=[pltpu.VMEM((classes, own), jnp.float32)] * n_src,
        in_specs=[SMEM] + [VMEM] * (4 + len(pieces)),
        out_specs=[VMEM] * n_src,
        scratch_shapes=scratch,
        compiler_params=GRANT,
    )(spot, *inside(high, low, w_in_t, w_out.T, *pieces))
    return to_owner(parts, n_src).T


def solution(mesh):
    in_specs = (
        P(("tgt", "src"), None),
        P("tgt", "src", None),
        P("tgt", "src"),
        P("tgt", "src", None, None, None),
        P(),
        P(),
    )
    out_specs = P(("tgt", "src"), None)
    return jax.shard_map(shards, mesh=mesh, in_specs=in_specs, out_specs=out_specs, check_vma=False)
```

```python
import functools

import jax
import jax.numpy as jnp
from jax import lax
from jax.experimental import pallas as pl
from jax.experimental.pallas import tpu as pltpu
from jax.sharding import PartitionSpec as P


VMEM = pl.BlockSpec(memory_space=pltpu.VMEM)
SMEM = pl.BlockSpec(memory_space=pltpu.SMEM)
GRANT = pltpu.CompilerParams(vmem_limit_bytes=24 << 20)
DIRECT = 4
DENSE_BYTES = 16 << 20


def inside(*arrays):
    return [pltpu.with_memory_space_constraint(array, pltpu.VMEM) for array in arrays]


def direct(size):
    return size <= DIRECT and not size & (size - 1)


def place_kernel(row_tiles, code_ref, tiles_ref, w_in_ref, high_ref, low_ref, w_in_t_ref):
    slots, tile, _ = tiles_ref.shape
    for slot in range(slots):
        values = tiles_ref[slot]
        high = values.astype(jnp.bfloat16).astype(jnp.float32)
        low = values - high
        code = jnp.full((tile, tile), code_ref[slot], jnp.int32)
        columns = slice(slot * tile, (slot + 1) * tile)
        for row in range(row_tiles):
            rows = slice(row * tile, (row + 1) * tile)
            here = code == row
            high_ref[rows, columns] = jnp.where(here, high, 0.0).astype(jnp.bfloat16)
            low_ref[rows, columns] = jnp.where(here, low, 0.0).astype(jnp.bfloat16)
    w_in_t_ref[...] = w_in_ref[...].T


def pick(spot_ref, pieces, joined_ref, picked_ref, tile):
    base = 0
    for piece in pieces:
        joined_ref[base : base + piece.shape[0], :] = piece[...]
        base += piece.shape[0]
    for slot in range(picked_ref.shape[0] // tile):
        start = pl.multiple_of(spot_ref[slot] * tile, tile)
        picked_ref[slot * tile : (slot + 1) * tile, :] = joined_ref[pl.ds(start, tile), :]


def rows_times(high_ref, low_ref, rows, columns, picked):
    return jnp.dot(high_ref[rows, columns], picked, preferred_element_type=jnp.float32) + jnp.dot(
        low_ref[rows, columns], picked, preferred_element_type=jnp.float32
    )


def times_transposed(left, right):
    return lax.dot_general(left, right, (((1,), (1,)), ((), ())), preferred_element_type=jnp.float32)


def times_rows(message, high_ref, low_ref, rows, columns):
    return times_transposed(message, high_ref[rows, columns]) + times_transposed(message, low_ref[rows, columns])


def transform(agg, w_in_t_ref, w_out_t_ref):
    hidden = jnp.maximum(times_transposed(w_in_t_ref[...], agg), 0.0).astype(jnp.bfloat16)
    return jnp.dot(w_out_t_ref[...], hidden, preferred_element_type=jnp.float32).astype(jnp.bfloat16)


def first_kernel(count, tile, spot_ref, high_ref, low_ref, *refs):
    pieces, outs, (joined_ref, picked_ref) = refs[:count], refs[count:-2], refs[-2:]
    pick(spot_ref, pieces, joined_ref, picked_ref, tile)
    picked, own = picked_ref[...], outs[0].shape[0]
    for d, out in enumerate(outs):
        out[...] = rows_times(high_ref, low_ref, slice(d * own, (d + 1) * own), slice(None), picked)


def second_kernel(count, tile, spot_ref, high_ref, low_ref, w_in_t_ref, w_out_t_ref, *refs):
    pieces, outs, (joined_ref, picked_ref) = refs[:count], refs[count:-2], refs[-2:]
    pick(spot_ref, pieces, joined_ref, picked_ref, tile)
    message = transform(picked_ref[...], w_in_t_ref, w_out_t_ref)
    own = outs[0].shape[1]
    for d, out in enumerate(outs):
        out[...] = times_rows(message, high_ref, low_ref, slice(d * own, (d + 1) * own), slice(None))


def place_dense_kernel(code_ref, spot_ref, tiles_ref, w_in_ref, high_ref, low_ref, w_in_t_ref):
    slots, tile, _ = tiles_ref.shape
    high_ref[...] = jnp.zeros_like(high_ref)
    low_ref[...] = jnp.zeros_like(low_ref)
    for slot in range(slots):

        @pl.when(code_ref[slot] >= 0)
        def _(slot=slot):
            values = tiles_ref[slot]
            high = values.astype(jnp.bfloat16)
            rows = pl.ds(pl.multiple_of(code_ref[slot] * tile, tile), tile)
            columns = pl.ds(pl.multiple_of(spot_ref[slot] * tile, tile), tile)
            high_ref[rows, columns] = high
            low_ref[rows, columns] = (values - high.astype(jnp.float32)).astype(jnp.bfloat16)

    w_in_t_ref[...] = w_in_ref[...].T


def columns_of(numbers, pieces):
    size = pieces[0].shape[0]
    return [slice(number * size, (number + 1) * size) for number in numbers]


def first_dense_kernel(numbers, rows, summed, high_ref, low_ref, *refs):
    before, pieces, out_ref = refs[:summed], refs[summed:-1], refs[-1]
    total = before[0][rows, :] if summed else None
    for columns, piece in zip(columns_of(numbers, pieces), pieces):
        term = rows_times(high_ref, low_ref, rows, columns, piece[...])
        total = term if total is None else total + term
    out_ref[...] = total


def second_dense_kernel(numbers, own, summed, high_ref, low_ref, w_in_t_ref, w_out_t_ref, *refs):
    count = len(numbers)
    before, pieces, outs = refs[:summed], refs[summed : summed + count], refs[summed + count :]
    message = transform(jnp.concatenate([piece[...] for piece in pieces], 0), w_in_t_ref, w_out_t_ref)
    size = pieces[0].shape[0]
    total = before[0][...] if summed else None
    for i, columns in enumerate(columns_of(numbers, pieces)):
        term = times_rows(message[:, i * size : (i + 1) * size], high_ref, low_ref, slice(None), columns)
        total = term if total is None else total + term
    for d, out in enumerate(outs):
        out[...] = total[:, d * own : d * own + out.shape[1]]


def exchange(value, groups):
    size = len(groups[0])
    if not direct(size):
        whole = lax.all_gather(value, "tgt", axis=0, axis_index_groups=groups)
        return [whole[i] for i in range(size)]
    moved = [value]
    for bits in range(1, size):
        pairs = [(group[i], group[i ^ bits]) for group in groups for i in range(size)]
        moved.append(lax.ppermute(value, "tgt", pairs))
    return moved


def spread(value, inner, outer):
    across = [[o * inner + i for o in range(outer)] for i in range(inner)]
    within = [[o * inner + i for i in range(inner)] for o in range(outer)]
    column = jnp.concatenate(exchange(value, across), 0)
    return exchange(column, within)


def place_of(size, mine, wanted):
    return wanted ^ mine if direct(size) else wanted


def to_owner(parts, n_src):
    moved = []
    for d, part in enumerate(parts, 1):
        pairs = [(i, (i + d) % n_src) for i in range(n_src)]
        moved.append(lax.ppermute(part, "src", pairs))
    return moved


def factors(n_tgt):
    inner = 1 << ((n_tgt.bit_length() - 1) // 2)
    return inner, n_tgt // inner


def layers(node_feats, tile_index, tile_count, tile_vals, w_in, w_out):
    tiles = tile_vals[0, 0]
    slots, tile, _ = tiles.shape
    own, width = node_feats.shape
    hidden_size, classes = w_out.shape
    n_src, n_tgt = lax.axis_size("src"), lax.axis_size("tgt")
    row_tiles, col_tiles = own * n_src // tile, own * n_tgt // tile
    per_own = own // tile
    inner, outer = factors(n_tgt)

    index, count = tile_index[0, 0], tile_count[0, 0]
    mine_t, mine_s = lax.axis_index("tgt"), lax.axis_index("src")
    turned = (index // col_tiles + row_tiles - mine_s * per_own) % row_tiles
    code = jnp.where(jnp.arange(slots) < count, turned, -1).astype(jnp.int32)
    column = index % col_tiles
    node, part = column // per_own, column % per_own
    in_spot = place_of(inner, mine_t % inner, node % inner)
    out_spot = place_of(outer, mine_t // inner, node // inner)
    spot = ((in_spot * outer + out_spot) * per_own + part).astype(jnp.int32)

    def call(kernel, outs, n_small, args, scratch=(), flops=0):
        return pl.pallas_call(
            kernel,
            out_shape=outs,
            in_specs=[SMEM] * n_small + [VMEM] * (len(args) - n_small),
            out_specs=jax.tree.map(lambda _: VMEM, outs),
            scratch_shapes=scratch,
            compiler_params=GRANT,
            cost_estimate=pl.CostEstimate(flops=flops, bytes_accessed=1 << 20, transcendentals=0),
        )(*args[:n_small], *inside(*args[n_small:]))

    all_rows, agg_part = row_tiles * tile, pltpu.VMEM((own, width), jnp.float32)
    out_part = pltpu.VMEM((classes, own), jnp.float32)
    w_in_shape, w_out_t = pltpu.VMEM(w_in.shape[::-1], w_in.dtype), w_out.T
    weights = 2 * (width * hidden_size + hidden_size * classes)
    pieces = spread(node_feats, inner, outer)

    if dense(n_src, n_tgt, own):
        placed = pltpu.VMEM((all_rows, own * n_tgt), jnp.bfloat16)
        high, low, w_in_t = call(place_dense_kernel, [placed, placed, w_in_shape], 2, (code, spot, tiles, w_in))
        depth = own * outer

        def first(numbers, rows, before):
            kernel = functools.partial(first_dense_kernel, numbers, rows, len(before))
            held = [pieces[number] for number in numbers]
            size = rows.stop - rows.start
            return call(
                kernel,
                pltpu.VMEM((size, width), jnp.float32),
                0,
                (high, low, *before, *held),
                (),
                4 * size * depth * width * len(held),
            )

        every = slice(0, all_rows)
        early = first((0,), every, ())
        early = first((3,), every, (early,))
        moved = to_owner([first((1, 2), slice(d * own, (d + 1) * own), (early,)) for d in range(1, n_src)], n_src)
        mine = first((1, 2), slice(0, own), (early,))
    else:
        depth = slots * tile
        placed = pltpu.VMEM((all_rows, depth), jnp.bfloat16)
        high, low, w_in_t = call(functools.partial(place_kernel, row_tiles), [placed, placed, w_in_shape], 1, (code, tiles, w_in))
        scratch = [pltpu.VMEM((own * n_tgt, width), jnp.bfloat16), pltpu.VMEM((depth, width), jnp.bfloat16)]
        mine, *others = call(
            functools.partial(first_kernel, len(pieces), tile),
            [agg_part] * n_src,
            1,
            (spot, high, low, *pieces),
            scratch,
            4 * all_rows * depth * width,
        )
        moved = to_owner(others, n_src)
    agg = sum(moved, mine).astype(jnp.bfloat16)

    pieces = spread(agg, inner, outer)
    if dense(n_src, n_tgt, own):

        def second(numbers, before, last):
            kernel = functools.partial(second_dense_kernel, numbers, own, len(before))
            held = [pieces[number] for number in numbers]
            return call(
                kernel,
                [out_part] * n_src if last else [pltpu.VMEM((classes, all_rows), jnp.float32)],
                0,
                (high, low, w_in_t, w_out_t, *before, *held),
                (),
                len(held) * depth * (weights + 4 * all_rows * classes),
            )

        early = second((0,), (), False)
        early = second((3,), early, False)
        mine, *others = second((1, 2), early, True)
    else:
        mine, *others = call(
            functools.partial(second_kernel, len(pieces), tile),
            [out_part] * n_src,
            1,
            (spot, high, low, w_in_t, w_out_t, *pieces),
            scratch,
            depth * (weights + 4 * all_rows * classes),
        )
    return sum(to_owner(others, n_src), mine).T


def dense(n_src, n_tgt, own):
    inner, outer = factors(n_tgt)
    return inner == outer == DIRECT and 4 * own * own * n_src * n_tgt <= DENSE_BYTES


def solution(mesh):
    in_specs = (
        P(("tgt", "src"), None),
        P("tgt", "src", None),
        P("tgt", "src"),
        P("tgt", "src", None, None, None),
        P(),
        P(),
    )
    out_specs = P(("tgt", "src"), None)
    return jax.shard_map(layers, mesh=mesh, in_specs=in_specs, out_specs=out_specs, check_vma=False)
```

```python
import functools

import jax
import jax.numpy as jnp
from jax import lax
from jax.experimental import pallas as pl
from jax.experimental.pallas import tpu as pltpu
from jax.sharding import PartitionSpec as P


VMEM = pl.BlockSpec(memory_space=pltpu.VMEM)
SMEM = pl.BlockSpec(memory_space=pltpu.SMEM)
GRANT = pltpu.CompilerParams(vmem_limit_bytes=24 << 20)
DIRECT = 4
CFG = {"p": ((3, 2, 1), {2: 1}, (3, 1, 2)), "s": ((3, 2, 1), {3: 1, 2: 2}, (3, 1, 2))}
EARLY, MIDDLE, LATE = ((0, True), (1, False), (2, False), (3, False)), ((3, True),), ((1, True), (2, True))


def inside(*arrays):
    return [pltpu.with_memory_space_constraint(array, pltpu.VMEM) for array in arrays]


def place_kernel(row_tiles, code_ref, tiles_ref, w_in_ref, high_ref, low_ref, w_in_t_ref):
    slots, tile, _ = tiles_ref.shape
    for slot in range(slots):
        values = tiles_ref[slot]
        high = values.astype(jnp.bfloat16).astype(jnp.float32)
        low = values - high
        code = jnp.full((tile, tile), code_ref[slot], jnp.int32)
        columns = slice(slot * tile, (slot + 1) * tile)
        for row in range(row_tiles):
            rows = slice(row * tile, (row + 1) * tile)
            here = code == row
            high_ref[rows, columns] = jnp.where(here, high, 0.0).astype(jnp.bfloat16)
            low_ref[rows, columns] = jnp.where(here, low, 0.0).astype(jnp.bfloat16)
    w_in_t_ref[...] = w_in_ref[...].T


def pick(spot_ref, pieces, joined_ref, picked_ref, tile):
    base = 0
    for piece in pieces:
        joined_ref[base : base + piece.shape[0], :] = piece[...]
        base += piece.shape[0]
    for slot in range(picked_ref.shape[0] // tile):
        start = pl.multiple_of(spot_ref[slot] * tile, tile)
        picked_ref[slot * tile : (slot + 1) * tile, :] = joined_ref[pl.ds(start, tile), :]


def rows_times(high_ref, low_ref, rows, columns, picked):
    return jnp.dot(high_ref[rows, columns], picked, preferred_element_type=jnp.float32) + jnp.dot(
        low_ref[rows, columns], picked, preferred_element_type=jnp.float32
    )


def times_transposed(left, right):
    return lax.dot_general(left, right, (((1,), (1,)), ((), ())), preferred_element_type=jnp.float32)


def times_rows(message, high_ref, low_ref, rows, columns):
    return times_transposed(message, high_ref[rows, columns]) + times_transposed(message, low_ref[rows, columns])


def transform(agg, w_in_t_ref, w_out_t_ref):
    hidden = jnp.maximum(times_transposed(w_in_t_ref[...], agg), 0.0).astype(jnp.bfloat16)
    return jnp.dot(w_out_t_ref[...], hidden, preferred_element_type=jnp.float32).astype(jnp.bfloat16)


def first_kernel(count, tile, spot_ref, high_ref, low_ref, *refs):
    pieces, outs, (joined_ref, picked_ref) = refs[:count], refs[count:-2], refs[-2:]
    pick(spot_ref, pieces, joined_ref, picked_ref, tile)
    picked, own = picked_ref[...], outs[0].shape[0]
    for d, out in enumerate(outs):
        out[...] = rows_times(high_ref, low_ref, slice(d * own, (d + 1) * own), slice(None), picked)


def second_kernel(count, tile, spot_ref, high_ref, low_ref, w_in_t_ref, w_out_t_ref, *refs):
    pieces, outs, (joined_ref, picked_ref) = refs[:count], refs[count:-2], refs[-2:]
    pick(spot_ref, pieces, joined_ref, picked_ref, tile)
    message = transform(picked_ref[...], w_in_t_ref, w_out_t_ref)
    own = outs[0].shape[1]
    for d, out in enumerate(outs):
        out[...] = times_rows(message, high_ref, low_ref, slice(d * own, (d + 1) * own), slice(None))


def place_dense_kernel(code_ref, spot_ref, tiles_ref, w_in_ref, high_ref, low_ref, w_in_t_ref):
    slots, tile, _ = tiles_ref.shape
    high_ref[...] = jnp.zeros_like(high_ref)
    low_ref[...] = jnp.zeros_like(low_ref)
    for slot in range(slots):

        @pl.when(code_ref[slot] >= 0)
        def _(slot=slot):
            values = tiles_ref[slot]
            high = values.astype(jnp.bfloat16)
            rows = pl.ds(pl.multiple_of(code_ref[slot] * tile, tile), tile)
            columns = pl.ds(pl.multiple_of(spot_ref[slot] * tile, tile), tile)
            high_ref[rows, columns] = high
            low_ref[rows, columns] = (values - high.astype(jnp.float32)).astype(jnp.bfloat16)

    w_in_t_ref[...] = w_in_ref[...].T


def first_dense_kernel(spans, rows, summed, high_ref, low_ref, *refs):
    before, pieces, out_ref = refs[:summed], refs[summed:-1], refs[-1]
    total = before[0][rows, :] if summed else None
    for columns, piece in zip(spans, pieces):
        term = rows_times(high_ref, low_ref, rows, columns, piece[...])
        total = term if total is None else total + term
    out_ref[...] = total


def second_dense_kernel(spans, own, summed, high_ref, low_ref, w_in_t_ref, w_out_t_ref, *refs):
    count = len(spans)
    before, pieces, outs = refs[:summed], refs[summed : summed + count], refs[summed + count :]
    message = transform(jnp.concatenate([piece[...] for piece in pieces], 0), w_in_t_ref, w_out_t_ref)
    total = before[0][...] if summed else None
    base = 0
    for columns in spans:
        size = columns.stop - columns.start
        term = times_rows(message[:, base : base + size], high_ref, low_ref, slice(None), columns)
        total = term if total is None else total + term
        base += size
    for d, out in enumerate(outs):
        out[...] = total[:, d * own : d * own + out.shape[1]]


def hop(value, groups, bits):
    pairs = [(group[i], group[i ^ bits]) for group in groups for i in range(len(group))]
    return lax.ppermute(value, "tgt", pairs)


def gather(value, groups):
    whole = lax.all_gather(value, "tgt", axis=0, axis_index_groups=groups)
    return [whole[i] for i in range(len(groups[0]))]


def spread(value, inner, outer, name):
    across = [[o * inner + i for o in range(outer)] for i in range(inner)]
    within = [[o * inner + i for i in range(inner)] for o in range(outer)]
    if not by_hops(inner, outer):
        return gather(jnp.concatenate(gather(value, across), 0), within)
    blocks = [value] + [hop(value, across, bits) for bits in (3, 2, 1)]
    column = jnp.concatenate(blocks, 0)
    pieces = [column]
    for bits in range(1, inner):
        split = CFG[name][1].get(bits, 0)
        if split:
            parts = [jnp.concatenate(part, 0) if len(part) > 1 else part[0] for part in (blocks[:split], blocks[split:])]
            pieces.append((hop(parts[0], within, bits), hop(parts[1], within, bits)))
        else:
            pieces.append(hop(column, within, bits))
    return pieces


def to_owner(parts, n_src):
    moved = []
    for d, part in enumerate(parts, 1):
        pairs = [(i, (i + d) % n_src) for i in range(n_src)]
        moved.append(lax.ppermute(part, "src", pairs))
    return moved


def factors(n_tgt):
    inner = 1 << ((n_tgt.bit_length() - 1) // 2)
    return inner, n_tgt // inner


def by_hops(inner, outer):
    return inner == outer == DIRECT


def layers(node_feats, tile_index, tile_count, tile_vals, w_in, w_out):
    tiles = tile_vals[0, 0]
    slots, tile, _ = tiles.shape
    own, width = node_feats.shape
    hidden_size, classes = w_out.shape
    n_src, n_tgt = lax.axis_size("src"), lax.axis_size("tgt")
    row_tiles, col_tiles = own * n_src // tile, own * n_tgt // tile
    per_own = own // tile
    inner, outer = factors(n_tgt)

    index, count = tile_index[0, 0], tile_count[0, 0]
    mine_t, mine_s = lax.axis_index("tgt"), lax.axis_index("src")
    turned = (index // col_tiles + row_tiles - mine_s * per_own) % row_tiles
    code = jnp.where(jnp.arange(slots) < count, turned, -1).astype(jnp.int32)
    column = index % col_tiles
    node, part = column // per_own, column % per_own
    in_spot, out_spot = node % inner, node // inner
    if by_hops(inner, outer):
        in_spot, out_spot = in_spot ^ (mine_t % inner), (outer - (out_spot ^ (mine_t // inner))) % outer
    spot = ((in_spot * outer + out_spot) * per_own + part).astype(jnp.int32)

    def call(kernel, outs, n_small, args, scratch=(), flops=0):
        return pl.pallas_call(
            kernel,
            out_shape=outs,
            in_specs=[SMEM] * n_small + [VMEM] * (len(args) - n_small),
            out_specs=jax.tree.map(lambda _: VMEM, outs),
            scratch_shapes=scratch,
            compiler_params=GRANT,
            cost_estimate=pl.CostEstimate(flops=flops, bytes_accessed=1 << 20, transcendentals=0),
        )(*args[:n_small], *inside(*args[n_small:]))

    all_rows, agg_part = row_tiles * tile, pltpu.VMEM((own, width), jnp.float32)
    out_part = pltpu.VMEM((classes, own), jnp.float32)
    w_in_shape, w_out_t = pltpu.VMEM(w_in.shape[::-1], w_in.dtype), w_out.T
    weights = 2 * (width * hidden_size + hidden_size * classes)
    pieces = spread(node_feats, inner, outer, "p")

    if by_hops(inner, outer):
        placed = pltpu.VMEM((all_rows, own * n_tgt), jnp.bfloat16)
        high, low, w_in_t = call(place_dense_kernel, [placed, placed, w_in_shape], 2, (code, spot, tiles, w_in))

        def pick_pieces(group):
            held, spans = [], []
            for number, late in group:
                parts = pieces[number] if isinstance(pieces[number], tuple) else (pieces[number],)
                base = number * own * outer
                for i, part in enumerate(parts):
                    if i == len(parts) - 1 if late else i < len(parts) - 1:
                        held.append(part)
                        spans.append(slice(base, base + part.shape[0]))
                    base += part.shape[0]
            return held, spans

        def first(numbers, rows, before):
            held, spans = pick_pieces(numbers)
            kernel = functools.partial(first_dense_kernel, spans, rows, len(before))
            size = rows.stop - rows.start
            return call(
                kernel,
                pltpu.VMEM((size, width), jnp.float32),
                0,
                (high, low, *before, *held),
                (),
                4 * size * own * outer * width,
            )

        every = slice(0, all_rows)
        early = first(EARLY, every, ())
        early = first(MIDDLE, every, (early,))
        others = [first(LATE, slice(d * own, (d + 1) * own), (early,)) for d in range(1, n_src)]
        moved = to_owner(others, n_src)
        mine = first(LATE, slice(0, own), (early,))
    else:
        depth = slots * tile
        placed = pltpu.VMEM((all_rows, depth), jnp.bfloat16)
        high, low, w_in_t = call(functools.partial(place_kernel, row_tiles), [placed, placed, w_in_shape], 1, (code, tiles, w_in))
        scratch = [pltpu.VMEM((own * n_tgt, width), jnp.bfloat16), pltpu.VMEM((depth, width), jnp.bfloat16)]
        mine, *others = call(
            functools.partial(first_kernel, len(pieces), tile),
            [agg_part] * n_src,
            1,
            (spot, high, low, *pieces),
            scratch,
            4 * all_rows * depth * width,
        )
        moved = to_owner(others, n_src)
    agg = sum(moved, mine).astype(jnp.bfloat16)

    pieces = spread(agg, inner, outer, "s")
    if by_hops(inner, outer):

        def second(numbers, before, last):
            held, spans = pick_pieces(numbers)
            kernel = functools.partial(second_dense_kernel, spans, own, len(before))
            return call(
                kernel,
                [out_part] * n_src if last else [pltpu.VMEM((classes, all_rows), jnp.float32)],
                0,
                (high, low, w_in_t, w_out_t, *before, *held),
                (),
                own * outer * (weights + 4 * all_rows * classes),
            )

        early = second(EARLY, (), False)
        early = second(MIDDLE, early, False)
        mine, *others = second(LATE, early, True)
    else:
        mine, *others = call(
            functools.partial(second_kernel, len(pieces), tile),
            [out_part] * n_src,
            1,
            (spot, high, low, w_in_t, w_out_t, *pieces),
            scratch,
            depth * (weights + 4 * all_rows * classes),
        )
    return sum(to_owner(others, n_src), mine).T


def solution(mesh):
    in_specs = (
        P(("tgt", "src"), None),
        P("tgt", "src", None),
        P("tgt", "src"),
        P("tgt", "src", None, None, None),
        P(),
        P(),
    )
    out_specs = P(("tgt", "src"), None)
    return jax.shard_map(layers, mesh=mesh, in_specs=in_specs, out_specs=out_specs, check_vma=False)
```

```python
import functools

import jax
import jax.numpy as jnp
from jax import lax
from jax.experimental import pallas as pl
from jax.experimental.pallas import tpu as pltpu
from jax.sharding import PartitionSpec as P


VMEM = pl.BlockSpec(memory_space=pltpu.VMEM)
SMEM = pl.BlockSpec(memory_space=pltpu.SMEM)
GRANT = pltpu.CompilerParams(vmem_limit_bytes=24 << 20)
DIRECT = 4
CFG = {"p": ((3, 2, 1), {2: 1}, (3, 1, 2)), "s": ((3, 1, 2), {3: 1, 2: 2}, (3, 1, 2))}
EARLY, MIDDLE, LATE = ((0, True), (1, False), (2, False), (3, False)), ((3, True),), ((1, True), (2, True))


def inside(*arrays):
    return [pltpu.with_memory_space_constraint(array, pltpu.VMEM) for array in arrays]


def place_kernel(row_tiles, code_ref, tiles_ref, w_in_ref, high_ref, low_ref, w_in_t_ref):
    slots, tile, _ = tiles_ref.shape
    for slot in range(slots):
        values = tiles_ref[slot]
        high = values.astype(jnp.bfloat16).astype(jnp.float32)
        low = values - high
        code = jnp.full((tile, tile), code_ref[slot], jnp.int32)
        columns = slice(slot * tile, (slot + 1) * tile)
        for row in range(row_tiles):
            rows = slice(row * tile, (row + 1) * tile)
            here = code == row
            high_ref[rows, columns] = jnp.where(here, high, 0.0).astype(jnp.bfloat16)
            low_ref[rows, columns] = jnp.where(here, low, 0.0).astype(jnp.bfloat16)
    w_in_t_ref[...] = w_in_ref[...].T


def pick(spot_ref, pieces, joined_ref, picked_ref, tile):
    base = 0
    for piece in pieces:
        joined_ref[base : base + piece.shape[0], :] = piece[...]
        base += piece.shape[0]
    for slot in range(picked_ref.shape[0] // tile):
        start = pl.multiple_of(spot_ref[slot] * tile, tile)
        picked_ref[slot * tile : (slot + 1) * tile, :] = joined_ref[pl.ds(start, tile), :]


def rows_times(high_ref, low_ref, rows, columns, picked):
    return jnp.dot(high_ref[rows, columns], picked, preferred_element_type=jnp.float32) + jnp.dot(
        low_ref[rows, columns], picked, preferred_element_type=jnp.float32
    )


def times_transposed(left, right):
    return lax.dot_general(left, right, (((1,), (1,)), ((), ())), preferred_element_type=jnp.float32)


def transform(agg, w_in_t_ref, w_out_t_ref):
    hidden = jnp.maximum(times_transposed(w_in_t_ref[...], agg), 0.0).astype(jnp.bfloat16)
    return jnp.dot(w_out_t_ref[...], hidden, preferred_element_type=jnp.float32).astype(jnp.bfloat16)


def first_kernel(count, tile, spot_ref, high_ref, low_ref, *refs):
    pieces, outs, (joined_ref, picked_ref) = refs[:count], refs[count:-2], refs[-2:]
    pick(spot_ref, pieces, joined_ref, picked_ref, tile)
    picked, own = picked_ref[...], outs[0].shape[0]
    for d, out in enumerate(outs):
        out[...] = rows_times(high_ref, low_ref, slice(d * own, (d + 1) * own), slice(None), picked)


def second_kernel(count, tile, spot_ref, high_ref, w_in_t_ref, w_out_t_ref, *refs):
    pieces, outs, (joined_ref, picked_ref) = refs[:count], refs[count:-2], refs[-2:]
    pick(spot_ref, pieces, joined_ref, picked_ref, tile)
    message = transform(picked_ref[...], w_in_t_ref, w_out_t_ref)
    own = outs[0].shape[1]
    for d, out in enumerate(outs):
        out[...] = times_transposed(message, high_ref[d * own : (d + 1) * own, :])


def place_dense_kernel(code_ref, spot_ref, tiles_ref, w_in_ref, high_ref, low_ref, w_in_t_ref):
    slots, tile, _ = tiles_ref.shape
    high_ref[...] = jnp.zeros_like(high_ref)
    low_ref[...] = jnp.zeros_like(low_ref)
    for slot in range(slots):

        @pl.when(code_ref[slot] >= 0)
        def _(slot=slot):
            values = tiles_ref[slot]
            high = values.astype(jnp.bfloat16)
            rows = pl.ds(pl.multiple_of(code_ref[slot] * tile, tile), tile)
            columns = pl.ds(pl.multiple_of(spot_ref[slot] * tile, tile), tile)
            high_ref[rows, columns] = high
            low_ref[rows, columns] = (values - high.astype(jnp.float32)).astype(jnp.bfloat16)

    w_in_t_ref[...] = w_in_ref[...].T


def first_dense_kernel(spans, rows, summed, high_ref, low_ref, *refs):
    before, pieces, out_ref = refs[:summed], refs[summed:-1], refs[-1]
    total = before[0][rows, :] if summed else None
    for columns, piece in zip(spans, pieces):
        term = rows_times(high_ref, low_ref, rows, columns, piece[...])
        total = term if total is None else total + term
    out_ref[...] = total


def second_dense_kernel(spans, own, summed, high_ref, w_in_t_ref, w_out_t_ref, *refs):
    count = len(spans)
    before, pieces, outs = refs[:summed], refs[summed : summed + count], refs[summed + count :]
    total = before[0][...] if summed else None
    message = transform(jnp.concatenate([piece[...] for piece in pieces], 0), w_in_t_ref, w_out_t_ref)
    base = 0
    for columns in spans:
        size = columns.stop - columns.start
        term = times_transposed(message[:, base : base + size], high_ref[:, columns])
        total = term if total is None else total + term
        base += size
    for d, out in enumerate(outs):
        out[...] = total[:, d * own : d * own + out.shape[1]]


def hop(value, groups, bits):
    pairs = [(group[i], group[i ^ bits]) for group in groups for i in range(len(group))]
    return lax.ppermute(value, "tgt", pairs)


def gather(value, groups):
    whole = lax.all_gather(value, "tgt", axis=0, axis_index_groups=groups)
    return [whole[i] for i in range(len(groups[0]))]


def spread(value, inner, outer, name):
    across = [[o * inner + i for o in range(outer)] for i in range(inner)]
    within = [[o * inner + i for i in range(inner)] for o in range(outer)]
    if not by_hops(inner, outer):
        return gather(jnp.concatenate(gather(value, across), 0), within)
    blocks = [value] + [hop(value, across, bits) for bits in (3, 2, 1)]
    column = jnp.concatenate(blocks, 0)
    pieces = [column]
    for bits in range(1, inner):
        split = CFG[name][1].get(bits, 0)
        if split:
            parts = [jnp.concatenate(part, 0) if len(part) > 1 else part[0] for part in (blocks[:split], blocks[split:])]
            pieces.append((hop(parts[0], within, bits), hop(parts[1], within, bits)))
        else:
            pieces.append(hop(column, within, bits))
    return pieces


def to_owner(parts, n_src):
    moved = []
    for d, part in enumerate(parts, 1):
        pairs = [(i, (i + d) % n_src) for i in range(n_src)]
        moved.append(lax.ppermute(part, "src", pairs))
    return moved


def factors(n_tgt):
    inner = 1 << ((n_tgt.bit_length() - 1) // 2)
    return inner, n_tgt // inner


def by_hops(inner, outer):
    return inner == outer == DIRECT


def layers(node_feats, tile_index, tile_count, tile_vals, w_in, w_out):
    tiles = tile_vals[0, 0]
    slots, tile, _ = tiles.shape
    own, width = node_feats.shape
    hidden_size, classes = w_out.shape
    n_src, n_tgt = lax.axis_size("src"), lax.axis_size("tgt")
    row_tiles, col_tiles = own * n_src // tile, own * n_tgt // tile
    per_own = own // tile
    inner, outer = factors(n_tgt)

    index, count = tile_index[0, 0], tile_count[0, 0]
    mine_t, mine_s = lax.axis_index("tgt"), lax.axis_index("src")
    turned = (index // col_tiles + row_tiles - mine_s * per_own) % row_tiles
    code = jnp.where(jnp.arange(slots) < count, turned, -1).astype(jnp.int32)
    column = index % col_tiles
    node, part = column // per_own, column % per_own
    in_spot, out_spot = node % inner, node // inner
    if by_hops(inner, outer):
        in_spot, out_spot = in_spot ^ (mine_t % inner), (outer - (out_spot ^ (mine_t // inner))) % outer
    spot = ((in_spot * outer + out_spot) * per_own + part).astype(jnp.int32)

    def call(kernel, outs, n_small, args, scratch=(), flops=0):
        return pl.pallas_call(
            kernel,
            out_shape=outs,
            in_specs=[SMEM] * n_small + [VMEM] * (len(args) - n_small),
            out_specs=jax.tree.map(lambda _: VMEM, outs),
            scratch_shapes=scratch,
            compiler_params=GRANT,
            cost_estimate=pl.CostEstimate(flops=flops, bytes_accessed=1 << 20, transcendentals=0),
        )(*args[:n_small], *inside(*args[n_small:]))

    all_rows, agg_part = row_tiles * tile, pltpu.VMEM((own, width), jnp.float32)
    out_part = pltpu.VMEM((classes, own), jnp.float32)
    w_in_shape, w_out_t = pltpu.VMEM(w_in.shape[::-1], w_in.dtype), w_out.T
    weights = 2 * (width * hidden_size + hidden_size * classes)
    pieces = spread(node_feats, inner, outer, "p")

    if by_hops(inner, outer):
        placed = pltpu.VMEM((all_rows, own * n_tgt), jnp.bfloat16)
        high, low, w_in_t = call(place_dense_kernel, [placed, placed, w_in_shape], 2, (code, spot, tiles, w_in))

        def pick_pieces(group):
            held, spans = [], []
            for number, late in group:
                parts = pieces[number] if isinstance(pieces[number], tuple) else (pieces[number],)
                base = number * own * outer
                for i, part in enumerate(parts):
                    if i == len(parts) - 1 if late else i < len(parts) - 1:
                        held.append(part)
                        spans.append(slice(base, base + part.shape[0]))
                    base += part.shape[0]
            return held, spans

        def first(numbers, rows, before):
            held, spans = pick_pieces(numbers)
            kernel = functools.partial(first_dense_kernel, spans, rows, len(before))
            size = rows.stop - rows.start
            return call(
                kernel,
                pltpu.VMEM((size, width), jnp.float32),
                0,
                (high, low, *before, *held),
                (),
                4 * size * own * outer * width,
            )

        every = slice(0, all_rows)
        early = first(EARLY, every, ())
        early = first(MIDDLE, every, (early,))
        others = [first(LATE, slice(d * own, (d + 1) * own), (early,)) for d in range(1, n_src)]
        moved = to_owner(others, n_src)
        mine = first(LATE, slice(0, own), (early,))
    else:
        depth = slots * tile
        placed = pltpu.VMEM((all_rows, depth), jnp.bfloat16)
        high, low, w_in_t = call(functools.partial(place_kernel, row_tiles), [placed, placed, w_in_shape], 1, (code, tiles, w_in))
        scratch = [pltpu.VMEM((own * n_tgt, width), jnp.bfloat16), pltpu.VMEM((depth, width), jnp.bfloat16)]
        mine, *others = call(
            functools.partial(first_kernel, len(pieces), tile),
            [agg_part] * n_src,
            1,
            (spot, high, low, *pieces),
            scratch,
            4 * all_rows * depth * width,
        )
        moved = to_owner(others, n_src)
    agg = sum(moved, mine).astype(jnp.bfloat16)

    pieces = spread(agg, inner, outer, "s")
    if by_hops(inner, outer):

        def second(numbers, before, last):
            held, spans = pick_pieces(numbers)
            kernel = functools.partial(second_dense_kernel, spans, own, len(before))
            return call(
                kernel,
                [out_part] * n_src if last else [pltpu.VMEM((classes, all_rows), jnp.float32)],
                0,
                (high, w_in_t, w_out_t, *before, *held),
                (),
                own * outer * (weights + 2 * all_rows * classes),
            )

        early = second(EARLY, (), False)
        early = second(MIDDLE, early, False)
        mine, *others = second(LATE, early, True)
    else:
        mine, *others = call(
            functools.partial(second_kernel, len(pieces), tile),
            [out_part] * n_src,
            1,
            (spot, high, w_in_t, w_out_t, *pieces),
            scratch,
            depth * (weights + 2 * all_rows * classes),
        )
    return sum(to_owner(others, n_src), mine).T


def solution(mesh):
    in_specs = (
        P(("tgt", "src"), None),
        P("tgt", "src", None),
        P("tgt", "src"),
        P("tgt", "src", None, None, None),
        P(),
        P(),
    )
    out_specs = P(("tgt", "src"), None)
    return jax.shard_map(layers, mesh=mesh, in_specs=in_specs, out_specs=out_specs, check_vma=False)
```

```python
import functools

import jax
import jax.numpy as jnp
from jax import lax
from jax.experimental import pallas as pl
from jax.experimental.pallas import tpu as pltpu
from jax.sharding import PartitionSpec as P


VMEM = pl.BlockSpec(memory_space=pltpu.VMEM)
SMEM = pl.BlockSpec(memory_space=pltpu.SMEM)
GRANT = pltpu.CompilerParams(vmem_limit_bytes=24 << 20)
DIRECT = 4
CFG = {"p": ((3, 2, 1), {2: 1}, (3, 1, 2)), "s": ((3, 2, 1), {3: 1, 2: 2}, (3, 1, 2))}
EARLY, MIDDLE, LATE = ((0, True), (1, False), (2, False), (3, False)), ((3, True),), ((1, True), (2, True))


def inside(*arrays):
    return [pltpu.with_memory_space_constraint(array, pltpu.VMEM) for array in arrays]


def place_kernel(row_tiles, code_ref, tiles_ref, w_in_ref, high_ref, low_ref, w_in_t_ref):
    slots, tile, _ = tiles_ref.shape
    for slot in range(slots):
        values = tiles_ref[slot]
        high = values.astype(jnp.bfloat16).astype(jnp.float32)
        low = values - high
        code = jnp.full((tile, tile), code_ref[slot], jnp.int32)
        columns = slice(slot * tile, (slot + 1) * tile)
        for row in range(row_tiles):
            rows = slice(row * tile, (row + 1) * tile)
            here = code == row
            high_ref[rows, columns] = jnp.where(here, high, 0.0).astype(jnp.bfloat16)
            low_ref[rows, columns] = jnp.where(here, low, 0.0).astype(jnp.bfloat16)
    w_in_t_ref[...] = w_in_ref[...].T


def pick(spot_ref, pieces, joined_ref, picked_ref, tile):
    base = 0
    for piece in pieces:
        joined_ref[base : base + piece.shape[0], :] = piece[...]
        base += piece.shape[0]
    for slot in range(picked_ref.shape[0] // tile):
        start = pl.multiple_of(spot_ref[slot] * tile, tile)
        picked_ref[slot * tile : (slot + 1) * tile, :] = joined_ref[pl.ds(start, tile), :]


def rows_times(high_ref, low_ref, rows, columns, picked):
    return jnp.dot(high_ref[rows, columns], picked, preferred_element_type=jnp.float32) + jnp.dot(
        low_ref[rows, columns], picked, preferred_element_type=jnp.float32
    )


def times_transposed(left, right):
    return lax.dot_general(left, right, (((1,), (1,)), ((), ())), preferred_element_type=jnp.float32)


def transform(agg, w_in_t_ref, w_out_t_ref):
    hidden = jnp.maximum(times_transposed(w_in_t_ref[...], agg), 0.0).astype(jnp.bfloat16)
    return jnp.dot(w_out_t_ref[...], hidden, preferred_element_type=jnp.float32).astype(jnp.bfloat16)


def first_kernel(count, tile, spot_ref, high_ref, low_ref, *refs):
    pieces, outs, (joined_ref, picked_ref) = refs[:count], refs[count:-2], refs[-2:]
    pick(spot_ref, pieces, joined_ref, picked_ref, tile)
    picked, own = picked_ref[...], outs[0].shape[0]
    for d, out in enumerate(outs):
        out[...] = rows_times(high_ref, low_ref, slice(d * own, (d + 1) * own), slice(None), picked)


def second_kernel(count, tile, spot_ref, high_ref, w_in_t_ref, w_out_t_ref, *refs):
    pieces, outs, (joined_ref, picked_ref) = refs[:count], refs[count:-2], refs[-2:]
    pick(spot_ref, pieces, joined_ref, picked_ref, tile)
    message = transform(picked_ref[...], w_in_t_ref, w_out_t_ref)
    own = outs[0].shape[1]
    for d, out in enumerate(outs):
        out[...] = times_transposed(message, high_ref[d * own : (d + 1) * own, :])


def place_dense_kernel(code_ref, spot_ref, tiles_ref, w_in_ref, high_ref, low_ref, w_in_t_ref):
    slots, tile, _ = tiles_ref.shape
    high_ref[...] = jnp.zeros_like(high_ref)
    low_ref[...] = jnp.zeros_like(low_ref)
    for slot in range(slots):

        @pl.when(code_ref[slot] >= 0)
        def _(slot=slot):
            values = tiles_ref[slot]
            high = values.astype(jnp.bfloat16)
            rows = pl.ds(pl.multiple_of(code_ref[slot] * tile, tile), tile)
            columns = pl.ds(pl.multiple_of(spot_ref[slot] * tile, tile), tile)
            high_ref[rows, columns] = high
            low_ref[rows, columns] = (values - high.astype(jnp.float32)).astype(jnp.bfloat16)

    w_in_t_ref[...] = w_in_ref[...].T


def first_dense_kernel(spans, rows, summed, high_ref, low_ref, *refs):
    before, pieces, out_ref = refs[:summed], refs[summed:-1], refs[-1]
    total = before[0][rows, :] if summed else None
    for columns, piece in zip(spans, pieces):
        term = rows_times(high_ref, low_ref, rows, columns, piece[...])
        total = term if total is None else total + term
    out_ref[...] = total


def second_dense_kernel(spans, own, summed, high_ref, w_in_t_ref, w_out_t_ref, *refs):
    count = len(spans)
    before, pieces, outs = refs[:summed], refs[summed : summed + count], refs[summed + count :]
    total = before[0][...] if summed else None
    message = transform(jnp.concatenate([piece[...] for piece in pieces], 0), w_in_t_ref, w_out_t_ref)
    base = 0
    for columns in spans:
        size = columns.stop - columns.start
        term = times_transposed(message[:, base : base + size], high_ref[:, columns])
        total = term if total is None else total + term
        base += size
    for d, out in enumerate(outs):
        out[...] = total[:, d * own : d * own + out.shape[1]]


def second_other_kernel(spans, own, high_ref, w_in_t_ref, w_out_t_ref, before_ref, *refs):
    count = len(spans)
    pieces, (message_ref, *outs) = refs[:count], refs[count:]
    message = transform(jnp.concatenate([piece[...] for piece in pieces], 0), w_in_t_ref, w_out_t_ref)
    message_ref[...] = message
    for d, out in enumerate(outs, 1):
        out[...] = before_ref[:, d * own : (d + 1) * own] + late_rows(message, high_ref, slice(d * own, (d + 1) * own), spans)


def second_own_kernel(spans, high_ref, before_ref, message_ref, out_ref):
    own = out_ref.shape[1]
    out_ref[...] = before_ref[:, :own] + late_rows(message_ref[...], high_ref, slice(0, own), spans)


def late_rows(message, high_ref, rows, spans):
    total, base = 0.0, 0
    for columns in spans:
        size = columns.stop - columns.start
        total = total + times_transposed(message[:, base : base + size], high_ref[rows, columns])
        base += size
    return total


def hop(value, groups, bits):
    pairs = [(group[i], group[i ^ bits]) for group in groups for i in range(len(group))]
    return lax.ppermute(value, "tgt", pairs)


def gather(value, groups):
    whole = lax.all_gather(value, "tgt", axis=0, axis_index_groups=groups)
    return [whole[i] for i in range(len(groups[0]))]


def spread(value, inner, outer, name):
    across = [[o * inner + i for o in range(outer)] for i in range(inner)]
    within = [[o * inner + i for i in range(inner)] for o in range(outer)]
    if not by_hops(inner, outer):
        return gather(jnp.concatenate(gather(value, across), 0), within)
    blocks = [value] + [hop(value, across, bits) for bits in (3, 2, 1)]
    column = jnp.concatenate(blocks, 0)
    pieces = [column]
    for bits in range(1, inner):
        split = CFG[name][1].get(bits, 0)
        if split:
            parts = [jnp.concatenate(part, 0) if len(part) > 1 else part[0] for part in (blocks[:split], blocks[split:])]
            pieces.append((hop(parts[0], within, bits), hop(parts[1], within, bits)))
        else:
            pieces.append(hop(column, within, bits))
    return pieces


def to_owner(parts, n_src):
    moved = []
    for d, part in enumerate(parts, 1):
        pairs = [(i, (i + d) % n_src) for i in range(n_src)]
        moved.append(lax.ppermute(part, "src", pairs))
    return moved


def factors(n_tgt):
    inner = 1 << ((n_tgt.bit_length() - 1) // 2)
    return inner, n_tgt // inner


def by_hops(inner, outer):
    return inner == outer == DIRECT


def layers(node_feats, tile_index, tile_count, tile_vals, w_in, w_out):
    tiles = tile_vals[0, 0]
    slots, tile, _ = tiles.shape
    own, width = node_feats.shape
    hidden_size, classes = w_out.shape
    n_src, n_tgt = lax.axis_size("src"), lax.axis_size("tgt")
    row_tiles, col_tiles = own * n_src // tile, own * n_tgt // tile
    per_own = own // tile
    inner, outer = factors(n_tgt)

    index, count = tile_index[0, 0], tile_count[0, 0]
    mine_t, mine_s = lax.axis_index("tgt"), lax.axis_index("src")
    turned = (index // col_tiles + row_tiles - mine_s * per_own) % row_tiles
    code = jnp.where(jnp.arange(slots) < count, turned, -1).astype(jnp.int32)
    column = index % col_tiles
    node, part = column // per_own, column % per_own
    in_spot, out_spot = node % inner, node // inner
    if by_hops(inner, outer):
        in_spot, out_spot = in_spot ^ (mine_t % inner), (outer - (out_spot ^ (mine_t // inner))) % outer
    spot = ((in_spot * outer + out_spot) * per_own + part).astype(jnp.int32)

    def call(kernel, outs, n_small, args, scratch=(), flops=0):
        return pl.pallas_call(
            kernel,
            out_shape=outs,
            in_specs=[SMEM] * n_small + [VMEM] * (len(args) - n_small),
            out_specs=jax.tree.map(lambda _: VMEM, outs),
            scratch_shapes=scratch,
            compiler_params=GRANT,
            cost_estimate=pl.CostEstimate(flops=flops, bytes_accessed=1 << 20, transcendentals=0),
        )(*args[:n_small], *inside(*args[n_small:]))

    all_rows, agg_part = row_tiles * tile, pltpu.VMEM((own, width), jnp.float32)
    out_part = pltpu.VMEM((classes, own), jnp.float32)
    w_in_shape, w_out_t = pltpu.VMEM(w_in.shape[::-1], w_in.dtype), w_out.T
    weights = 2 * (width * hidden_size + hidden_size * classes)
    pieces = spread(node_feats, inner, outer, "p")

    if by_hops(inner, outer):
        placed = pltpu.VMEM((all_rows, own * n_tgt), jnp.bfloat16)
        high, low, w_in_t = call(place_dense_kernel, [placed, placed, w_in_shape], 2, (code, spot, tiles, w_in))

        def pick_pieces(group):
            held, spans = [], []
            for number, late in group:
                parts = pieces[number] if isinstance(pieces[number], tuple) else (pieces[number],)
                base = number * own * outer
                for i, part in enumerate(parts):
                    if i == len(parts) - 1 if late else i < len(parts) - 1:
                        held.append(part)
                        spans.append(slice(base, base + part.shape[0]))
                    base += part.shape[0]
            return held, spans

        def first(numbers, rows, before):
            held, spans = pick_pieces(numbers)
            kernel = functools.partial(first_dense_kernel, spans, rows, len(before))
            size = rows.stop - rows.start
            return call(
                kernel,
                pltpu.VMEM((size, width), jnp.float32),
                0,
                (high, low, *before, *held),
                (),
                4 * size * own * outer * width,
            )

        every = slice(0, all_rows)
        early = first(EARLY, every, ())
        early = first(MIDDLE, every, (early,))
        others = [first(LATE, slice(d * own, (d + 1) * own), (early,)) for d in range(1, n_src)]
        moved = to_owner(others, n_src)
        mine = first(LATE, slice(0, own), (early,))
    else:
        depth = slots * tile
        placed = pltpu.VMEM((all_rows, depth), jnp.bfloat16)
        high, low, w_in_t = call(functools.partial(place_kernel, row_tiles), [placed, placed, w_in_shape], 1, (code, tiles, w_in))
        scratch = [pltpu.VMEM((own * n_tgt, width), jnp.bfloat16), pltpu.VMEM((depth, width), jnp.bfloat16)]
        mine, *others = call(
            functools.partial(first_kernel, len(pieces), tile),
            [agg_part] * n_src,
            1,
            (spot, high, low, *pieces),
            scratch,
            4 * all_rows * depth * width,
        )
        moved = to_owner(others, n_src)
    agg = sum(moved, mine).astype(jnp.bfloat16)

    pieces = spread(agg, inner, outer, "s")
    if by_hops(inner, outer):

        def second(numbers, before, last):
            held, spans = pick_pieces(numbers)
            kernel = functools.partial(second_dense_kernel, spans, own, len(before))
            return call(
                kernel,
                [out_part] * n_src if last else [pltpu.VMEM((classes, all_rows), jnp.float32)],
                0,
                (high, w_in_t, w_out_t, *before, *held),
                (),
                own * outer * (weights + 2 * all_rows * classes),
            )

        early = second(EARLY, (), False)
        early = second(MIDDLE, early, False)
        held, spans = pick_pieces(LATE)
        size = sum(columns.stop - columns.start for columns in spans)
        message, *others = call(
            functools.partial(second_other_kernel, spans, own),
            [pltpu.VMEM((classes, size), jnp.bfloat16)] + [out_part] * (n_src - 1),
            0,
            (high, w_in_t, w_out_t, *early, *held),
            (),
            size * (weights + 2 * own * classes),
        )
        others = to_owner(others, n_src)
        mine = call(
            functools.partial(second_own_kernel, spans), out_part, 0, (high, *early, message), (), 2 * size * own * classes
        )
    else:
        mine, *others = call(
            functools.partial(second_kernel, len(pieces), tile),
            [out_part] * n_src,
            1,
            (spot, high, w_in_t, w_out_t, *pieces),
            scratch,
            depth * (weights + 2 * all_rows * classes),
        )
        others = to_owner(others, n_src)
    return sum(others, mine).T


def solution(mesh):
    in_specs = (
        P(("tgt", "src"), None),
        P("tgt", "src", None),
        P("tgt", "src"),
        P("tgt", "src", None, None, None),
        P(),
        P(),
    )
    out_specs = P(("tgt", "src"), None)
    return jax.shard_map(layers, mesh=mesh, in_specs=in_specs, out_specs=out_specs, check_vma=False)
```
